32 devices in a mesh: dp: 8 (over z, y), fsdp: 4 (over x, core).
Axes of the slice: x: 2, y: 2, z: 4, core: 2. Of those that a mesh axis runs over, the one named last changes fastest.
Arguments:
- adapter_token_input: bfloat16 [512, 32, 4096], P('dp', None, 'fsdp'), may hold values from -6 to 6
- output_gradient_rows: bfloat16 [512, 32, 2048], P('dp', None, 'fsdp'), may hold values from -6 to 6
- adapter_down_weight: bfloat16 [64, 4096], P(None, 'fsdp'), may hold values from -0.09375 to 0.09375
- real_token_count: int32 [512], P('dp'), may hold values from 1 to 32, 10240 in all
- projection: bfloat16 [131072, 4096], P('fsdp', 'dp'), may hold values from -0.015625 to 0.015625
- targets: bfloat16 [256, 4096], P(None, 'dp'), may hold values from -6 to 6
Outputs:
- scores: float32 [512, 256], P('fsdp', 'dp')
The draws below stay inside these ranges and needn't reach their ends.
Inputs may be any that keep to these rules, and one draw needn't show every extreme that they name: real_token_count[e] counts the real positions of example e, from position 0; the counts sum to 10240 and the largest equals 32.
All inputs are finite; a program needn't handle non-finite values. No bound on the sum of `real_token_count` on one device may be relied on, other than what follows from the above.
Results may differ from the reference program's by a relative error of at most 0.0042.
Values may be sent and summed in bfloat16 or wider, within the bound.
No kernel may reach another device: no remote copies, remote signals or barrier semaphores. Data moves between devices by JAX's collectives and lax.ppermute only.
A program may use at most 192 MiB of HBM per device.

```python
import math
import jax
import jax.numpy as jnp
import numpy as np
from jax import lax

MODEL_WIDTH = 4096
OUT_WIDTH = 2048
ADAPTER_RANK = 64
K = 4096
TOKEN_LENGTH = 32
NTGT = 256
POOL_EXAMPLES = 512
GRAD = 131072


def block_levels(own_key, extent, split, least, high):
    level, own = 1.0, jax.random.fold_in(own_key, 6)
    for dim, parts in split:
        steps = jnp.exp(jax.random.uniform(jax.random.fold_in(own, dim), (parts,), jnp.float32, least / len(split), high / len(split)))
        level = level * jnp.repeat(steps, extent[dim] // parts).reshape([-1 if axis == dim else 1 for axis in range(len(extent))])
    return level


def profile(amount, total, most, skew):
    weights = [(1 << 20) // math.isqrt(standing ** skew) + 1 for standing in range(2, amount + 1)]
    surplus, counts = total - most - (amount - 1), [1] * (amount - 1)
    while surplus > 0:
        free = [i for i in range(amount - 1) if counts[i] < most]
        mass, remaining = sum([weights[i] for i in free]), surplus
        for i in free:
            extra = min(most - counts[i], max(1, remaining * weights[i] // mass), surplus)
            counts[i] = counts[i] + extra
            surplus = surplus - extra
    return np.array([most] + counts)


def uneven_parts(stream_key, amount, total, bound, slope):
    if amount == 2:
        one = jax.random.randint(stream_key, (), max(1, total - bound), min(bound, total - 1) + 1)
        return jnp.stack([one, total - one])
    lengths = jnp.asarray(profile(amount, total, bound, slope), jnp.int32)
    pairs = (amount - 1) // 2
    giver, sink = lengths[1:1 + 2 * pairs:2], lengths[2:2 + 2 * pairs:2]
    room = jnp.minimum(giver - 1, bound - sink)
    shifted = jax.random.randint(jax.random.fold_in(stream_key, 1), (pairs,), 0, 1 << 20) % (room + 1)
    lengths = lengths.at[1:1 + 2 * pairs:2].set(giver - shifted).at[2:2 + 2 * pairs:2].set(sink + shifted)
    return lengths[jax.random.permutation(jax.random.fold_in(stream_key, 2), amount)]


def scatter_about(stream_key, dims, spread, most, split=(), held_as=jnp.bfloat16):
    values = jax.random.normal(stream_key, dims, jnp.float32) * spread
    if len(split) > 0:
        values = block_levels(stream_key, dims, split, -0.22, 0.18) * values
    return jnp.clip(values, min=-most, max=most).astype(held_as)


def setup_inputs(seed: int = 0) -> dict:
    seeds = jax.random.split(jax.random.key(seed), 7)
    adapter_token_input = scatter_about(seeds[0], (POOL_EXAMPLES, TOKEN_LENGTH, MODEL_WIDTH), 1.0, 6.0, ((0, 8), (2, 4)))
    output_gradient_rows = scatter_about(seeds[1], (POOL_EXAMPLES, TOKEN_LENGTH, OUT_WIDTH), 1.0, 6.0, ((0, 8), (2, 4)))
    adapter_down_weight = scatter_about(seeds[2], (ADAPTER_RANK, MODEL_WIDTH), MODEL_WIDTH ** -0.5, 0.09375, ((1, 4),))
    real_token_count = uneven_parts(seeds[3], POOL_EXAMPLES, POOL_EXAMPLES * TOKEN_LENGTH * 5 // 8, TOKEN_LENGTH, 0).astype(jnp.int32)
    projection = scatter_about(seeds[4], (GRAD, K), GRAD ** -0.5, 0.015625, ((0, 4), (1, 8)))
    targets = scatter_about(seeds[5], (NTGT, K), 1.0, 6.0, ((1, 8),))
    return dict(adapter_token_input=adapter_token_input, output_gradient_rows=output_gradient_rows, adapter_down_weight=adapter_down_weight, real_token_count=real_token_count, projection=projection, targets=targets)


def reference(adapter_token_input, output_gradient_rows, adapter_down_weight, real_token_count, projection, targets):
    flattened_rows = adapter_token_input.reshape(POOL_EXAMPLES * TOKEN_LENGTH, MODEL_WIDTH)
    adapter_rank_float = jnp.dot(flattened_rows, adapter_down_weight.T, preferred_element_type=jnp.float32).reshape(POOL_EXAMPLES, TOKEN_LENGTH, ADAPTER_RANK)
    positions = jnp.arange(TOKEN_LENGTH, dtype=jnp.int32)
    keep = (positions[None, :] < real_token_count[:, None]).astype(jnp.float32)
    rank_acts = (adapter_rank_float * keep[:, :, None]).astype(jnp.bfloat16)

    def one_grad(pair):
        grad_rows, acts_rows = pair
        return jnp.dot(grad_rows.T, acts_rows, preferred_element_type=jnp.float32).astype(jnp.bfloat16).reshape(OUT_WIDTH * ADAPTER_RANK)
    grads = lax.map(one_grad, (output_gradient_rows, rank_acts))
    features = jnp.dot(grads, projection, preferred_element_type=jnp.float32)
    pool_unit = features / jnp.sqrt(lax.optimization_barrier(jnp.sum(features * features, axis=1, keepdims=True)) + 1e-06)
    target_f = targets.astype(jnp.float32)
    target_unit = target_f / jnp.sqrt(lax.optimization_barrier(jnp.sum(target_f * target_f, axis=1, keepdims=True)) + 1e-06)
    cosines = jnp.dot(pool_unit, target_unit.T, precision=lax.Precision.HIGHEST, preferred_element_type=jnp.float32)
    return cosines * jnp.sqrt(jnp.float32(K))
```

```python
import functools

import jax
import jax.numpy as jnp
import numpy as np
from jax import lax
from jax.experimental import pallas as pl
from jax.experimental.pallas import tpu as pltpu
from jax.sharding import PartitionSpec as P

F32 = jnp.float32
BF16 = jnp.bfloat16
LANES = 128
VMEM_LIMIT = 34 * 1024 * 1024


def ring_order(n):
    ny = 2
    while ny * ny * 4 <= n:
        ny *= 2
    nz = n // ny
    path = []
    for z in range(nz):
        ys = range(1, ny) if z % 2 == 0 else range(ny - 1, 0, -1)
        path += [z * ny + y for y in ys]
    return path + [z * ny for z in reversed(range(nz))]


def form_project_kernel(dims, meta, *refs):
    shards, parts, row, pool, rank, pairs, block, first_row = dims
    g_refs = [refs[k * parts : (k + 1) * parts] for k in range(shards)]
    a_refs = refs[shards * parts : shards * (parts + 1)]
    p_hbm, acc_hbm, out_hbm, pbuf, s_ref, held, p_sems, acc_sems = refs[shards * (parts + 1) :]
    blocks = pairs // block
    rows = block * rank
    width = 1 + 2 * pool
    stride = shards * pool + 8

    def p_copy(i, h):
        start = pl.multiple_of(first_row + (h * pairs + i * block) * rank, rank)
        return pltpu.make_async_copy(
            p_hbm.at[pl.ds(start, rows)], pbuf.at[i, h], p_sems.at[i, h]
        )

    def acc_rows(k):
        return pl.ds(pl.multiple_of(meta[(row + k) * width] * pool, pool), pool)

    def acc_load(k):
        return pltpu.make_async_copy(
            acc_hbm.at[acc_rows(k)], held.at[pl.ds(k * pool, pool)], acc_sems.at[0, k]
        )

    def acc_store(k):
        return pltpu.make_async_copy(
            held.at[pl.ds(k * pool, pool)], out_hbm.at[acc_rows(k)], acc_sems.at[1, k]
        )

    for i in range(blocks):
        for h in range(2):
            p_copy(i, h).start()
    for k in range(shards):
        acc_load(k).start()
    tiles = a_refs[0].shape[1] // LANES
    low = lax.broadcasted_iota(jnp.int32, (pairs, LANES), 1) < rank
    lane = lax.broadcasted_iota(jnp.int32, (rank, 2 * LANES), 1)

    for k in range(shards):
        first = (row + k) * width + 1

        def two_examples(p, carry, k=k, first=first):
            e = 2 * p
            tile = jnp.minimum(meta[first + e] // LANES, tiles - 2)
            base = pl.multiple_of(tile * LANES, LANES)
            g = jnp.concatenate([g_ref[:, pl.ds(base, 2 * LANES)] for g_ref in g_refs[k]], axis=0)
            a = a_refs[k][:, pl.ds(base, 2 * LANES)]
            masked = []
            for j in range(2):
                begin = meta[first + e + j] - base
                end = begin + meta[first + pool + e + j]
                part = jnp.where((lane >= begin) & (lane < end), a, jnp.zeros_like(a))
                masked += [part, part]
            formed = lax.dot_general(
                g,
                jnp.concatenate(masked, axis=0),
                (((1,), (1,)), ((), ())),
                preferred_element_type=F32,
            )
            for j in range(2):
                own = formed[:, j * LANES : (j + 1) * LANES]
                s_ref[pl.ds(k * pool + e + j, pairs, stride=stride), :] = jnp.where(
                    low, own[:pairs], own[pairs:]
                )
            return carry

        lax.fori_loop(0, pool // 2, two_examples, 0, unroll=4)
    for k in range(shards):
        acc_load(k).wait()

    def project(i, carry):
        p_copy(i, 0).wait()
        p_copy(i, 1).wait()
        left = jnp.concatenate(
            [
                s_ref[pl.ds(pl.multiple_of((i * block + o) * stride, 8), shards * pool), :].astype(BF16)
                for o in range(block)
            ],
            axis=1,
        )
        right = jnp.concatenate(
            [
                pbuf[i, h, pl.ds(o * rank, rank), :]
                for o in range(block)
                for h in range(2)
            ],
            axis=0,
        )
        held[...] += jnp.dot(left, right, preferred_element_type=F32)
        return carry

    lax.fori_loop(0, blocks, project, 0)
    for k in range(shards):
        acc_store(k).start()
    for k in range(shards):
        acc_store(k).wait()


def form_project(acc, meta, row, gs, acts, projection, half, pool):
    shards, parts = len(gs), len(gs[0])
    outs = parts * gs[0][0].shape[0]
    rank, room = acts[0].shape
    feats = projection.shape[1]
    pairs = outs // 2
    block = min(16, pairs)
    dims = (shards, parts, row, pool, rank, pairs, block, half * outs * rank)
    whole = lambda x: pl.BlockSpec(x.shape, lambda i, m: (0, 0))
    flat = [g for group in gs for g in group]
    spec = pltpu.PrefetchScalarGridSpec(
        num_scalar_prefetch=1,
        grid=(1,),
        in_specs=[whole(x) for x in flat + list(acts)]
        + [pl.BlockSpec(memory_space=pl.ANY)] * 2,
        out_specs=pl.BlockSpec(memory_space=pl.ANY),
        scratch_shapes=[
            pltpu.VMEM((pairs // block, 2, block * rank, feats), BF16),
            pltpu.VMEM((pairs * (shards * pool + 8), LANES), F32),
            pltpu.VMEM((shards * pool, feats), F32),
            pltpu.SemaphoreType.DMA((pairs // block, 2)),
            pltpu.SemaphoreType.DMA((2, shards)),
        ],
    )
    return pl.pallas_call(
        functools.partial(form_project_kernel, dims),
        out_shape=jax.ShapeDtypeStruct(acc.shape, F32),
        grid_spec=spec,
        input_output_aliases={len(flat) + shards + 2: 0},
        compiler_params=pltpu.CompilerParams(vmem_limit_bytes=VMEM_LIMIT),
        cost_estimate=pl.CostEstimate(
            flops=2 * shards * pool * outs * rank * feats,
            bytes_accessed=outs * rank * feats * 2,
            transcendentals=0,
        ),
        name="form_project",
    )(meta, *flat, *acts, projection, acc)


def exchange_sum(x, axis, n):
    me = lax.axis_index(axis)
    bit = 1
    slots = x[:, None]
    while bit < n:
        swap = [(i, i ^ bit) for i in range(n)]
        mine = (me // bit) % 2
        grouped = slots.reshape((slots.shape[0] // 2, 2) + x.shape[1:])
        keep = lax.dynamic_index_in_dim(grouped, mine, 1, keepdims=False)
        send = lax.dynamic_index_in_dim(grouped, 1 - mine, 1, keepdims=False)
        slots = keep + lax.ppermute(send, axis, swap)
        bit *= 2
    return slots.reshape(x.shape[1:])


def exchange_total(x, axis, n, bit=1):
    while bit < n:
        x = x + lax.ppermute(x, axis, [(i, i ^ bit) for i in range(n)])
        bit *= 2
    return x


def per_device(dp, fsdp, tokens, grad_rows, down, counts, projection, targets):
    pool, length, width = tokens.shape
    outs = grad_rows.shape[2]
    rank = down.shape[0]
    feats = projection.shape[1]
    half = outs // 2
    room = -(-3 * pool * length // (4 * LANES)) * LANES
    before = jnp.arange(pool)[None, :] < jnp.arange(pool)[:, None]
    starts = jnp.sum(jnp.where(before, counts[None, :], 0), axis=1)
    t = jnp.arange(length, dtype=jnp.int32)[None, :]
    place = jnp.where(t < counts[:, None], starts[:, None] + t, -1).reshape(pool * length)
    select = (place[:, None] == jnp.arange(room, dtype=jnp.int32)[None, :]).astype(BF16)
    packed = lax.dot_general(
        grad_rows.reshape(pool * length, outs),
        select,
        (((0,), (0,)), ((), ())),
        preferred_element_type=F32,
    ).astype(BF16)

    me = lax.axis_index("dp")
    order = ring_order(dp)
    ahead = [(order[i], order[(i + 1) % dp]) for i in range(dp)]
    back = [(b, a) for a, b in ahead]
    swap = [(i, i ^ 1) for i in range(fsdp)]
    core = lax.axis_index("fsdp") % 2

    acts_part = lax.dot_general(
        down,
        tokens.reshape(pool * length, width),
        (((1,), (1,)), ((), ())),
        preferred_element_type=F32,
    ).reshape(2, rank // 2, pool * length)
    keep = lax.dynamic_index_in_dim(acts_part, core, 0, keepdims=False)
    send = lax.dynamic_index_in_dim(acts_part, 1 - core, 0, keepdims=False)
    acts_half = exchange_total(keep + lax.ppermute(send, "fsdp", swap), "fsdp", fsdp, 2)
    real = (place >= 0).astype(F32)[None, :]
    acts_half = (acts_half * real).astype(BF16)

    def both_halves(mine):
        other = lax.ppermute(mine, "fsdp", swap)
        return jnp.where(
            core == 0,
            jnp.concatenate([mine, other], axis=0),
            jnp.concatenate([other, mine], axis=0),
        )

    own_acts = both_halves(
        jnp.dot(acts_half, select, preferred_element_type=F32).astype(BF16)
    )

    own = jnp.concatenate([starts, counts])
    table = lax.dynamic_update_slice(jnp.zeros((dp, 2 * pool), jnp.int32), own[None], (me, 0))
    table, packed = lax.optimization_barrier((exchange_total(table, "dp", dp), packed))
    overflow = jnp.max(jnp.sum(table[:, pool:], axis=1)) > room
    my_position = jnp.asarray(np.argsort(order), jnp.int32)[me]
    blocks = jnp.asarray(order, jnp.int32)[(my_position - jnp.arange(dp + 1)) % dp]
    meta = jnp.concatenate([blocks[:, None], table[blocks]], axis=1).reshape(-1)

    acts = {0: own_acts, dp: own_acts}
    low, high = {0: packed[:half]}, {0: packed[half:]}
    acc = jnp.zeros((dp * pool, feats), F32)
    for s in range(dp):
        if s > 0:
            keys = [k for k in (s, dp - s) if k in acts]
            low[s], high[s], acc, *fresh = lax.optimization_barrier(
                (low[s], high[s], acc, *[acts[k] for k in keys])
            )
            acts.update(zip(keys, fresh))
        if s + 1 < dp:
            low[s + 1] = lax.ppermute(low[s], "dp", ahead)
            high[s + 1] = lax.ppermute(high[s], "dp", back)
        if 2 * (s + 1) <= dp:
            acts[s + 1] = lax.ppermute(acts[s], "dp", ahead)
        if 2 * (s + 1) < dp:
            acts[dp - s - 1] = lax.ppermute(acts[dp - s], "dp", back)
        if s % 2 == 1:
            rows = [s - 1, s]
            acc = form_project(
                acc, meta, s - 1, [[low[i]] for i in rows], [acts[i] for i in rows],
                projection, 0, pool,
            )
        if s > 0 and (s % 2 == 0 or s == dp - 1):
            rows = [s - s % 2, s - s % 2 + 1] if s == dp - 1 else [s - 2, s - 1]
            rows = [dp - rows[1], dp - rows[0]]
            acc = form_project(
                acc, meta, rows[0], [[high[dp - i]] for i in rows], [acts[i] for i in rows],
                projection, 1, pool,
            )

    def padded(acc):
        mine = both_halves(acts_half).reshape(rank, pool, length)
        grads = jnp.einsum("elo,rel->eor", grad_rows, mine, preferred_element_type=F32)
        grads = grads.astype(BF16).reshape(pool, outs * rank)
        grads = lax.all_gather(grads, "dp", axis=0, tiled=True)
        return jnp.dot(grads, projection, preferred_element_type=F32)

    acc = lax.cond(overflow, padded, lambda acc: acc, acc)
    pooled = exchange_sum(acc.reshape(fsdp, dp * pool // fsdp, feats), "fsdp", fsdp)
    target_f = targets.astype(F32)
    queries = targets.shape[0]
    share = queries // dp
    rows = pooled.shape[0]
    raw = lax.dot_general(
        target_f,
        pooled,
        (((1,), (1,)), ((), ())),
        precision=lax.Precision.HIGHEST,
        preferred_element_type=F32,
    ).reshape(dp, share, rows)
    pool_sq = jnp.sum(pooled * pooled, axis=1)
    target_sq = jnp.sum(target_f * target_f, axis=1).reshape(dp, 1, share)
    sent = jnp.concatenate(
        [
            raw,
            jnp.broadcast_to(pool_sq[None, None, :], (dp, 1, rows)),
            jnp.pad(target_sq, ((0, 0), (0, 0), (0, rows - share))),
        ],
        axis=1,
    )
    got = jnp.sum(lax.all_to_all(sent, "dp", 0, 0), axis=0)
    pool_norm = jnp.sqrt(got[share] + 1e-06)
    target_norm = jnp.sqrt(got[share + 1, :share] + 1e-06)
    scale = jnp.sqrt(F32(feats * dp))
    return (got[:share].T / pool_norm[:, None]) / target_norm[None, :] * scale


def solution(mesh):
    dp, fsdp = mesh.shape["dp"], mesh.shape["fsdp"]
    return jax.shard_map(
        functools.partial(per_device, dp, fsdp),
        mesh=mesh,
        in_specs=(
            P("dp", None, "fsdp"),
            P("dp", None, "fsdp"),
            P(None, "fsdp"),
            P("dp"),
            P("fsdp", "dp"),
            P(None, "dp"),
        ),
        out_specs=P("fsdp", "dp"),
        check_vma=False,
    )
```

```python
import functools

import jax
import jax.numpy as jnp
import numpy as np
from jax import lax
from jax.experimental import pallas as pl
from jax.experimental.pallas import tpu as pltpu
from jax.sharding import PartitionSpec as P

F32 = jnp.float32
BF16 = jnp.bfloat16
LANES = 128
VMEM_LIMIT = 34 * 1024 * 1024


def ring_order(n):
    ny = 2
    while ny * ny * 4 <= n:
        ny *= 2
    nz = n // ny
    path = []
    for z in range(nz):
        ys = range(1, ny) if z % 2 == 0 else range(ny - 1, 0, -1)
        path += [z * ny + y for y in ys]
    return path + [z * ny for z in reversed(range(nz))]


def form_project_kernel(dims, blocks_ref, *refs):
    shards, row, pool, rank, pairs, block, first_row = dims
    g_refs, a_refs = refs[:shards], refs[shards : 2 * shards]
    p_hbm, acc_hbm, out_hbm, pbuf, s_ref, held, words, meta, p_sems, acc_sems = refs[2 * shards :]
    blocks = pairs // block
    rows = block * rank
    stride = shards * pool + 8
    room = g_refs[0].shape[1]

    def p_copy(i, h):
        start = pl.multiple_of(first_row + (h * pairs + i * block) * rank, rank)
        return pltpu.make_async_copy(
            p_hbm.at[pl.ds(start, rows)], pbuf.at[i, h], p_sems.at[i, h]
        )

    def acc_rows(k):
        return pl.ds(pl.multiple_of(blocks_ref[row + k] * pool, pool), pool)

    def acc_load(k):
        return pltpu.make_async_copy(
            acc_hbm.at[acc_rows(k)], held.at[pl.ds(k * pool, pool)], acc_sems.at[0, k]
        )

    def acc_store(k):
        return pltpu.make_async_copy(
            held.at[pl.ds(k * pool, pool)], out_hbm.at[acc_rows(k)], acc_sems.at[1, k]
        )

    for i in range(blocks):
        for h in range(2):
            p_copy(i, h).start()
    for k in range(shards):
        acc_load(k).start()
        words[k] = a_refs[k][: 2 * 8, room:].astype(F32).astype(jnp.int32)
    to_scalars = [
        pltpu.make_async_copy(words.at[k, pl.ds(0, 8)], meta.at[k], acc_sems.at[2, k])
        for k in range(shards)
    ]
    for copy in to_scalars:
        copy.start()
    tiles = room // LANES
    low = lax.broadcasted_iota(jnp.int32, (pairs, LANES), 1) < rank
    lane = lax.broadcasted_iota(jnp.int32, (rank, 2 * LANES), 1)

    for k in range(shards):
        to_scalars[k].wait()

        def two_examples(p, carry, k=k):
            e = 2 * p
            tile = jnp.minimum(meta[k, 1, e], tiles - 2)
            base = pl.multiple_of(tile * LANES, LANES)
            g = g_refs[k][:, pl.ds(base, 2 * LANES)]
            a = a_refs[k][:, pl.ds(base, 2 * LANES)]
            masked = []
            for j in range(2):
                begin = meta[k, 1, e + j] * LANES + meta[k, 2, e + j] - base
                end = begin + meta[k, 0, e + j]
                part = jnp.where((lane >= begin) & (lane < end), a, jnp.zeros_like(a))
                masked += [part, part]
            formed = lax.dot_general(
                g,
                jnp.concatenate(masked, axis=0),
                (((1,), (1,)), ((), ())),
                preferred_element_type=F32,
            )
            for j in range(2):
                own = formed[:, j * LANES : (j + 1) * LANES]
                s_ref[pl.ds(k * pool + e + j, pairs, stride=stride), :] = jnp.where(
                    low, own[:pairs], own[pairs:]
                )
            return carry

        lax.fori_loop(0, pool // 2, two_examples, 0, unroll=4)
    for k in range(shards):
        acc_load(k).wait()

    def project(i, carry):
        p_copy(i, 0).wait()
        p_copy(i, 1).wait()
        left = jnp.concatenate(
            [
                s_ref[pl.ds(pl.multiple_of((i * block + o) * stride, 8), shards * pool), :].astype(BF16)
                for o in range(block)
            ],
            axis=1,
        )
        right = jnp.concatenate(
            [
                pbuf[i, h, pl.ds(o * rank, rank), :]
                for o in range(block)
                for h in range(2)
            ],
            axis=0,
        )
        held[...] += jnp.dot(left, right, preferred_element_type=F32)
        return carry

    lax.fori_loop(0, blocks, project, 0)
    for k in range(shards):
        acc_store(k).start()
    for k in range(shards):
        acc_store(k).wait()


def form_project(acc, blocks, row, gs, acts, projection, half, pool):
    shards = len(gs)
    outs = gs[0].shape[0]
    rank = acts[0].shape[0]
    feats = projection.shape[1]
    pairs = outs // 2
    block = min(16, pairs)
    dims = (shards, row, pool, rank, pairs, block, half * outs * rank)
    whole = lambda x: pl.BlockSpec(x.shape, lambda i, m: (0, 0))
    flat = list(gs)
    spec = pltpu.PrefetchScalarGridSpec(
        num_scalar_prefetch=1,
        grid=(1,),
        in_specs=[whole(x) for x in flat + list(acts)]
        + [pl.BlockSpec(memory_space=pl.ANY)] * 2,
        out_specs=pl.BlockSpec(memory_space=pl.ANY),
        scratch_shapes=[
            pltpu.VMEM((pairs // block, 2, block * rank, feats), BF16),
            pltpu.VMEM(((pairs + 1) * (shards * pool + 8), LANES), F32),
            pltpu.VMEM((shards * pool, feats), F32),
            pltpu.VMEM((shards, 16, LANES), jnp.int32),
            pltpu.SMEM((shards, 8, LANES), jnp.int32),
            pltpu.SemaphoreType.DMA((pairs // block, 2)),
            pltpu.SemaphoreType.DMA((3, shards)),
        ],
    )
    return pl.pallas_call(
        functools.partial(form_project_kernel, dims),
        out_shape=jax.ShapeDtypeStruct(acc.shape, F32),
        grid_spec=spec,
        input_output_aliases={len(flat) + shards + 2: 0},
        compiler_params=pltpu.CompilerParams(vmem_limit_bytes=VMEM_LIMIT),
        cost_estimate=pl.CostEstimate(
            flops=2 * shards * pool * outs * rank * feats,
            bytes_accessed=outs * rank * feats * 2,
            transcendentals=0,
        ),
        name="form_project",
    )(blocks, *flat, *acts, projection, acc)


def exchange_sum(x, axis, n):
    me = lax.axis_index(axis)
    bit = 1
    slots = x[:, None]
    while bit < n:
        swap = [(i, i ^ bit) for i in range(n)]
        mine = (me // bit) % 2
        grouped = slots.reshape((slots.shape[0] // 2, 2) + x.shape[1:])
        keep = lax.dynamic_index_in_dim(grouped, mine, 1, keepdims=False)
        send = lax.dynamic_index_in_dim(grouped, 1 - mine, 1, keepdims=False)
        slots = keep + lax.ppermute(send, axis, swap)
        bit *= 2
    return slots.reshape(x.shape[1:])


def exchange_total(x, axis, n, bit=1):
    while bit < n:
        x = x + lax.ppermute(x, axis, [(i, i ^ bit) for i in range(n)])
        bit *= 2
    return x


def per_device(dp, fsdp, tokens, grad_rows, down, counts, projection, targets):
    pool, length, width = tokens.shape
    outs = grad_rows.shape[2]
    rank = down.shape[0]
    feats = projection.shape[1]
    half = outs // 2
    room = -(-3 * pool * length // (4 * LANES)) * LANES
    before = jnp.arange(pool)[None, :] < jnp.arange(pool)[:, None]
    starts = jnp.sum(jnp.where(before, counts[None, :], 0), axis=1)
    t = jnp.arange(length, dtype=jnp.int32)[None, :]
    place = jnp.where(t < counts[:, None], starts[:, None] + t, -1).reshape(pool * length)
    select = (place[:, None] == jnp.arange(room, dtype=jnp.int32)[None, :]).astype(BF16)
    packed = lax.dot_general(
        grad_rows.reshape(pool * length, outs),
        select,
        (((0,), (0,)), ((), ())),
        preferred_element_type=F32,
    ).astype(BF16)

    me = lax.axis_index("dp")
    order = ring_order(dp)
    ahead = [(order[i], order[(i + 1) % dp]) for i in range(dp)]
    back = [(b, a) for a, b in ahead]
    swap = [(i, i ^ 1) for i in range(fsdp)]
    core = lax.axis_index("fsdp") % 2

    acts_part = lax.dot_general(
        down,
        tokens.reshape(pool * length, width),
        (((1,), (1,)), ((), ())),
        preferred_element_type=F32,
    ).reshape(2, rank // 2, pool * length)
    keep = lax.dynamic_index_in_dim(acts_part, core, 0, keepdims=False)
    send = lax.dynamic_index_in_dim(acts_part, 1 - core, 0, keepdims=False)
    acts_half = exchange_total(keep + lax.ppermute(send, "fsdp", swap), "fsdp", fsdp, 2)
    real = (place >= 0).astype(F32)[None, :]
    acts_half = (acts_half * real).astype(BF16)

    def both_halves(mine):
        other = lax.ppermute(mine, "fsdp", swap)
        return jnp.where(
            core == 0,
            jnp.concatenate([mine, other], axis=0),
            jnp.concatenate([other, mine], axis=0),
        )

    words = jnp.stack([counts, starts // LANES, starts % LANES]).astype(BF16)
    words = jnp.pad(words, ((0, rank // 2 - 3), (0, -pool % LANES)))
    own_half = jnp.dot(acts_half, select, preferred_element_type=F32).astype(BF16)
    own_acts = both_halves(jnp.concatenate([own_half, words], axis=1))
    my_position = jnp.asarray(np.argsort(order), jnp.int32)[me]
    blocks = jnp.asarray(order, jnp.int32)[(my_position - jnp.arange(dp + 1)) % dp]

    acts = {0: own_acts, dp: own_acts}
    low, high = {0: packed[:half]}, {dp: packed[half:]}
    acc = jnp.zeros((dp * pool, feats), F32)

    def add(acc, first, gs, which):
        return form_project(
            acc, blocks, first, [gs[first], gs[first + 1]], [acts[first], acts[first + 1]],
            projection, which, pool,
        )

    for s in range(dp):
        if s > 0:
            keys = [k for k in dict.fromkeys((s, dp - s)) if k in acts]
            low[s], high[dp - s], acc, *fresh = lax.optimization_barrier(
                (low[s], high[dp - s], acc, *[acts[k] for k in keys])
            )
            acts.update(zip(keys, fresh))
        if s + 1 < dp:
            low[s + 1] = lax.ppermute(low[s], "dp", ahead)
            high[dp - s - 1] = lax.ppermute(high[dp - s], "dp", back)
        if 2 * (s + 1) <= dp:
            acts[s + 1] = lax.ppermute(acts[s], "dp", ahead)
        if 2 * (s + 1) < dp:
            acts[dp - s - 1] = lax.ppermute(acts[dp - s], "dp", back)
        if s % 2 == 1:
            acc = add(acc, s - 1, low, 0)
        if s > 0 and s % 2 == 0:
            acc = add(acc, dp - s + 1, high, 1)
        if s == dp - 1:
            acc = add(acc, 1, high, 1)

    used = jnp.stack([acts[i][0, room : room + pool] for i in range(dp)]).astype(jnp.int32)
    overflow = jnp.max(jnp.sum(used, axis=1)) > room

    def padded(acc):
        mine = both_halves(acts_half).reshape(rank, pool, length)
        grads = jnp.einsum("elo,rel->eor", grad_rows, mine, preferred_element_type=F32)
        grads = grads.astype(BF16).reshape(pool, outs * rank)

        def step(s, state):
            acc, grads = state
            part = jnp.dot(grads, projection, preferred_element_type=F32)
            block = lax.dynamic_index_in_dim(blocks, s, 0, keepdims=False)
            acc = lax.dynamic_update_slice(acc, part, (block * pool, 0))
            return acc, lax.ppermute(grads, "dp", ahead)

        return lax.fori_loop(0, dp, step, (acc, grads))[0]

    acc = lax.cond(overflow, padded, lambda acc: acc, acc)
    pooled = exchange_sum(acc.reshape(fsdp, dp * pool // fsdp, feats), "fsdp", fsdp)
    target_f = targets.astype(F32)
    queries = targets.shape[0]
    share = queries // dp
    rows = pooled.shape[0]
    raw = lax.dot_general(
        target_f,
        pooled,
        (((1,), (1,)), ((), ())),
        precision=lax.Precision.HIGHEST,
        preferred_element_type=F32,
    ).reshape(dp, share, rows)
    pool_sq = jnp.sum(pooled * pooled, axis=1)
    target_sq = jnp.sum(target_f * target_f, axis=1).reshape(dp, 1, share)
    sent = jnp.concatenate(
        [
            raw,
            jnp.broadcast_to(pool_sq[None, None, :], (dp, 1, rows)),
            jnp.pad(target_sq, ((0, 0), (0, 0), (0, rows - share))),
        ],
        axis=1,
    )
    got = jnp.sum(lax.all_to_all(sent, "dp", 0, 0), axis=0)
    pool_norm = jnp.sqrt(got[share] + 1e-06)
    target_norm = jnp.sqrt(got[share + 1, :share] + 1e-06)
    scale = jnp.sqrt(F32(feats * dp))
    return (got[:share].T / pool_norm[:, None]) / target_norm[None, :] * scale


def solution(mesh):
    dp, fsdp = mesh.shape["dp"], mesh.shape["fsdp"]
    return jax.shard_map(
        functools.partial(per_device, dp, fsdp),
        mesh=mesh,
        in_specs=(
            P("dp", None, "fsdp"),
            P("dp", None, "fsdp"),
            P(None, "fsdp"),
            P("dp"),
            P("fsdp", "dp"),
            P(None, "dp"),
        ),
        out_specs=P("fsdp", "dp"),
        check_vma=False,
    )
```

```python
import functools

import jax
import jax.numpy as jnp
import numpy as np
from jax import lax
from jax.experimental import pallas as pl
from jax.experimental.pallas import tpu as pltpu
from jax.sharding import PartitionSpec as P

F32 = jnp.float32
BF16 = jnp.bfloat16
LANES = 128
VMEM_LIMIT = 34 * 1024 * 1024


def ring_order(n):
    ny = 2
    while ny * ny * 4 <= n:
        ny *= 2
    nz = n // ny
    path = []
    for z in range(nz):
        ys = range(1, ny) if z % 2 == 0 else range(ny - 1, 0, -1)
        path += [z * ny + y for y in ys]
    return path + [z * ny for z in reversed(range(nz))]


def form_project_kernel(dims, blocks_ref, *refs):
    shards, row, pool, rank, pairs, block, first_row, last = dims
    g_refs, own_refs, other_refs = (refs[i * shards : (i + 1) * shards] for i in range(3))
    p_hbm, acc_hbm, out_hbm, pbuf, s_ref, held, words, meta, p_sems, acc_sems = refs[3 * shards :]
    blocks = pairs // block
    rows = block * rank
    stride = shards * pool + 8
    room = g_refs[0].shape[1]

    def p_copy(i, h):
        start = pl.multiple_of(first_row + (h * pairs + i * block) * rank, rank)
        return pltpu.make_async_copy(
            p_hbm.at[pl.ds(start, rows)], pbuf.at[i, h], p_sems.at[i, h]
        )

    def acc_rows(k):
        return pl.ds(pl.multiple_of(blocks_ref[row + k] * pool, pool), pool)

    def acc_load(k):
        return pltpu.make_async_copy(
            acc_hbm.at[acc_rows(k)], held.at[pl.ds(k * pool, pool)], acc_sems.at[0, k]
        )

    def acc_store(k):
        return pltpu.make_async_copy(
            held.at[pl.ds(k * pool, pool)], out_hbm.at[acc_rows(k)], acc_sems.at[1, k]
        )

    for i in range(blocks):
        for h in range(2):
            p_copy(i, h).start()
    for k in range(shards):
        acc_load(k).start()
        words[k] = own_refs[k][: 2 * 8, room:].astype(F32).astype(jnp.int32)
    to_scalars = [
        pltpu.make_async_copy(words.at[k, pl.ds(0, 8)], meta.at[k], acc_sems.at[2, k])
        for k in range(shards)
    ]
    for copy in to_scalars:
        copy.start()
    tiles = room // LANES
    low = lax.broadcasted_iota(jnp.int32, (pairs, LANES), 1) < rank
    lane = lax.broadcasted_iota(jnp.int32, (rank, 2 * LANES), 1)
    first_core = jnp.full((rank // 2, 2 * LANES), blocks_ref[blocks_ref.shape[0] - 1]) == 0

    for k in range(shards):
        to_scalars[k].wait()

        def two_examples(p, carry, k=k):
            e = 2 * p
            tile = jnp.minimum(meta[k, 1, e], tiles - 2)
            base = pl.multiple_of(tile * LANES, LANES)
            g = g_refs[k][:, pl.ds(base, 2 * LANES)]
            own = own_refs[k][:, pl.ds(base, 2 * LANES)]
            other = other_refs[k][:, pl.ds(base, 2 * LANES)]
            a = jnp.concatenate(
                [jnp.where(first_core, own, other), jnp.where(first_core, other, own)], axis=0
            )
            masked = []
            for j in range(2):
                begin = meta[k, 1, e + j] * LANES + meta[k, 2, e + j] - base
                end = begin + meta[k, 0, e + j]
                part = jnp.where((lane >= begin) & (lane < end), a, jnp.zeros_like(a))
                masked += [part, part]
            formed = lax.dot_general(
                g,
                jnp.concatenate(masked, axis=0),
                (((1,), (1,)), ((), ())),
                preferred_element_type=F32,
            )
            for j in range(2):
                own = formed[:, j * LANES : (j + 1) * LANES]
                s_ref[pl.ds(k * pool + e + j, pairs, stride=stride), :] = jnp.where(
                    low, own[:pairs], own[pairs:]
                )
            return carry

        lax.fori_loop(0, pool // 2, two_examples, 0, unroll=8 if last else 4)
    for k in range(shards):
        acc_load(k).wait()

    def project(i, carry):
        p_copy(i, 0).wait()
        p_copy(i, 1).wait()
        left = jnp.concatenate(
            [
                s_ref[
                    pl.ds(pl.multiple_of((i * block + o) * stride, 8), shards * pool), :
                ].astype(BF16)
                for o in range(block)
            ],
            axis=1,
        )
        right = jnp.concatenate(
            [
                pbuf[i, h, pl.ds(o * rank, rank), :]
                for o in range(block)
                for h in range(2)
            ],
            axis=0,
        )
        held[...] += jnp.dot(left, right, preferred_element_type=F32)
        return carry

    lax.fori_loop(0, blocks, project, 0, unroll=blocks if last else 1)
    for k in range(shards):
        acc_store(k).start()
    for k in range(shards):
        acc_store(k).wait()


def form_project(acc, blocks, row, gs, acts, projection, half, pool, last):
    shards = len(gs)
    outs = gs[0].shape[0]
    rank = 2 * acts[0][0].shape[0]
    feats = projection.shape[1]
    pairs = outs // 2
    block = min(32, pairs)
    dims = (shards, row, pool, rank, pairs, block, half * outs * rank, last)
    whole = lambda x: pl.BlockSpec(x.shape, lambda i, m: (0, 0))
    flat = list(gs) + [a[0] for a in acts] + [a[1] for a in acts]
    spec = pltpu.PrefetchScalarGridSpec(
        num_scalar_prefetch=1,
        grid=(1,),
        in_specs=[whole(x) for x in flat]
        + [pl.BlockSpec(memory_space=pl.ANY)] * 2,
        out_specs=pl.BlockSpec(memory_space=pl.ANY),
        scratch_shapes=[
            pltpu.VMEM((pairs // block, 2, block * rank, feats), BF16),
            pltpu.VMEM(((pairs + 1) * (shards * pool + 8), LANES), F32),
            pltpu.VMEM((shards * pool, feats), F32),
            pltpu.VMEM((shards, 16, LANES), jnp.int32),
            pltpu.SMEM((shards, 8, LANES), jnp.int32),
            pltpu.SemaphoreType.DMA((pairs // block, 2)),
            pltpu.SemaphoreType.DMA((3, shards)),
        ],
    )
    return pl.pallas_call(
        functools.partial(form_project_kernel, dims),
        out_shape=jax.ShapeDtypeStruct(acc.shape, F32),
        grid_spec=spec,
        input_output_aliases={len(flat) + 2: 0},
        compiler_params=pltpu.CompilerParams(vmem_limit_bytes=VMEM_LIMIT),
        cost_estimate=pl.CostEstimate(
            flops=2 * shards * pool * outs * rank * feats,
            bytes_accessed=outs * rank * feats * 2,
            transcendentals=0,
        ),
        name="form_project",
    )(blocks, *flat, projection, acc)


def exchange_sum(x, axis, n):
    me = lax.axis_index(axis)
    bit = 1
    slots = x[:, None]
    while bit < n:
        swap = [(i, i ^ bit) for i in range(n)]
        mine = (me // bit) % 2
        grouped = slots.reshape((slots.shape[0] // 2, 2) + x.shape[1:])
        keep = lax.dynamic_index_in_dim(grouped, mine, 1, keepdims=False)
        send = lax.dynamic_index_in_dim(grouped, 1 - mine, 1, keepdims=False)
        if bit > 1:
            send = send.astype(BF16)
        slots = keep + lax.ppermute(send, axis, swap).astype(F32)
        bit *= 2
    return slots.reshape(x.shape[1:])


def exchange_total(x, axis, n, bit=1):
    while bit < n:
        x = x + lax.ppermute(x, axis, [(i, i ^ bit) for i in range(n)])
        bit *= 2
    return x


def per_device(dp, fsdp, tokens, grad_rows, down, counts, projection, targets):
    pool, length, width = tokens.shape
    outs = grad_rows.shape[2]
    rank = down.shape[0]
    feats = projection.shape[1]
    half = outs // 2
    room = -(-3 * pool * length // (4 * LANES)) * LANES
    before = jnp.arange(pool)[None, :] < jnp.arange(pool)[:, None]
    starts = jnp.sum(jnp.where(before, counts[None, :], 0), axis=1)
    t = jnp.arange(length, dtype=jnp.int32)[None, :]
    place = jnp.where(t < counts[:, None], starts[:, None] + t, -1).reshape(pool * length)
    select = (place[:, None] == jnp.arange(room, dtype=jnp.int32)[None, :]).astype(BF16)
    packed = lax.dot_general(
        grad_rows.reshape(pool * length, outs),
        select,
        (((0,), (0,)), ((), ())),
        preferred_element_type=F32,
    ).astype(BF16)

    me = lax.axis_index("dp")
    order = ring_order(dp)
    ahead = [(order[i], order[(i + 1) % dp]) for i in range(dp)]
    back = [(b, a) for a, b in ahead]
    swap = [(i, i ^ 1) for i in range(fsdp)]
    core = lax.axis_index("fsdp") % 2

    acts_part = lax.dot_general(
        down,
        tokens.reshape(pool * length, width),
        (((1,), (1,)), ((), ())),
        preferred_element_type=F32,
    ).reshape(2, rank // 2, pool * length)
    keep = lax.dynamic_index_in_dim(acts_part, core, 0, keepdims=False)
    send = lax.dynamic_index_in_dim(acts_part, 1 - core, 0, keepdims=False)
    acts_half = exchange_total(keep + lax.ppermute(send, "fsdp", swap), "fsdp", fsdp, 2)
    real = (place >= 0).astype(F32)[None, :]
    acts_half = (acts_half * real).astype(BF16)

    def both_halves(mine):
        other = lax.ppermute(mine, "fsdp", swap)
        return jnp.where(
            core == 0,
            jnp.concatenate([mine, other], axis=0),
            jnp.concatenate([other, mine], axis=0),
        )

    words = jnp.stack([counts, starts // LANES, starts % LANES]).astype(BF16)
    words = jnp.pad(words, ((0, rank // 2 - 3), (0, -pool % LANES)))
    own_half = jnp.dot(acts_half, select, preferred_element_type=F32).astype(BF16)
    own_half = jnp.concatenate([own_half, words], axis=1)
    my_position = jnp.asarray(np.argsort(order), jnp.int32)[me]
    blocks = jnp.asarray(order, jnp.int32)[(my_position - jnp.arange(dp + 1)) % dp]
    blocks = jnp.concatenate([blocks, core[None].astype(jnp.int32)])

    halves = {0: own_half, dp: own_half}
    acts = {}
    low, high = {0: packed[:half]}, {dp: packed[half:]}
    acc = jnp.zeros((dp * pool, feats), F32)
    overflow = None

    blocks, acc = lax.optimization_barrier((blocks, acc))

    def add(acc, blocks, first, gs, which):
        return form_project(
            acc, blocks, first, [gs[first], gs[first + 1]], [acts[first], acts[first + 1]],
            projection, which, pool, first in (1, dp - 2),
        )

    for s in range(dp):
        keys = [k for k in dict.fromkeys((s, dp - s)) if k in halves]
        if s == dp // 2 + 1:
            used = jnp.stack([halves[i][0, room : room + pool] for i in range(dp)])
            overflow = jnp.max(jnp.sum(used.astype(jnp.int32), axis=1)) > room
            low[s], high[dp - s], acc, overflow = lax.optimization_barrier(
                (low[s], high[dp - s], acc, overflow)
            )
        elif s > 0:
            low[s], high[dp - s], acc, blocks, *fresh = lax.optimization_barrier(
                (low[s], high[dp - s], acc, blocks, *[halves[k] for k in keys])
            )
            halves.update(zip(keys, fresh))
        if s + 1 < dp:
            low[s + 1] = lax.ppermute(low[s], "dp", ahead)
            high[dp - s - 1] = lax.ppermute(high[dp - s], "dp", back)
        if 2 * (s + 1) <= dp:
            halves[s + 1] = lax.ppermute(halves[s], "dp", ahead)
        if 2 * (s + 1) < dp:
            halves[dp - s - 1] = lax.ppermute(halves[dp - s], "dp", back)
        for k in keys:
            acts[k] = acts[0] if k == dp else (halves[k], lax.ppermute(halves[k], "fsdp", swap))
        if s % 2 == 1:
            acc = add(acc, blocks, s - 1, low, 0)
        if s > 0 and s % 2 == 0:
            acc = add(acc, blocks, dp - s + 1, high, 1)
        if s == dp - 1:
            acc = add(acc, blocks, 1, high, 1)

    def padded(acc):
        mine = both_halves(acts_half).reshape(rank, pool, length)
        grads = jnp.einsum("elo,rel->eor", grad_rows, mine, preferred_element_type=F32)
        grads = grads.astype(BF16).reshape(pool, outs * rank)

        def step(s, state):
            acc, grads = state
            part = jnp.dot(grads, projection, preferred_element_type=F32)
            block = lax.dynamic_index_in_dim(blocks, s, 0, keepdims=False)
            acc = lax.dynamic_update_slice(acc, part, (block * pool, 0))
            return acc, lax.ppermute(grads, "dp", ahead)

        return lax.fori_loop(0, dp, step, (acc, grads))[0]

    acc = lax.cond(overflow, padded, lambda acc: acc, acc)
    pooled = exchange_sum(acc.reshape(fsdp, dp * pool // fsdp, feats), "fsdp", fsdp)
    target_f = targets.astype(F32)
    queries = targets.shape[0]
    share = queries // dp
    rows = pooled.shape[0]
    raw = lax.dot_general(
        target_f,
        pooled,
        (((1,), (1,)), ((), ())),
        precision=lax.Precision.HIGHEST,
        preferred_element_type=F32,
    ).reshape(dp, share, rows)
    pool_sq = jnp.sum(pooled * pooled, axis=1)
    target_sq = jnp.sum(target_f * target_f, axis=1).reshape(dp, 1, share)
    sent = jnp.concatenate(
        [
            raw,
            jnp.broadcast_to(pool_sq[None, None, :], (dp, 1, rows)),
            jnp.pad(target_sq, ((0, 0), (0, 0), (0, rows - share))),
        ],
        axis=1,
    )
    got = jnp.sum(lax.all_to_all(sent, "dp", 0, 0), axis=0)
    pool_norm = jnp.sqrt(got[share] + 1e-06)
    target_norm = jnp.sqrt(got[share + 1, :share] + 1e-06)
    scale = jnp.sqrt(F32(feats * dp))
    return (got[:share].T / pool_norm[:, None]) / target_norm[None, :] * scale


def solution(mesh):
    dp, fsdp = mesh.shape["dp"], mesh.shape["fsdp"]
    return jax.shard_map(
        functools.partial(per_device, dp, fsdp),
        mesh=mesh,
        in_specs=(
            P("dp", None, "fsdp"),
            P("dp", None, "fsdp"),
            P(None, "fsdp"),
            P("dp"),
            P("fsdp", "dp"),
            P(None, "dp"),
        ),
        out_specs=P("fsdp", "dp"),
        check_vma=False,
    )
```

```python
import functools

import jax
import jax.numpy as jnp
import numpy as np
from jax import lax
from jax.experimental import pallas as pl
from jax.experimental.pallas import tpu as pltpu
from jax.sharding import PartitionSpec as P

F32 = jnp.float32
BF16 = jnp.bfloat16
LANES = 128
VMEM_LIMIT = 34 * 1024 * 1024


def ring_order(n):
    ny = 2
    while ny * ny * 4 <= n:
        ny *= 2
    nz = n // ny
    path = []
    for z in range(nz):
        ys = range(1, ny) if z % 2 == 0 else range(ny - 1, 0, -1)
        path += [z * ny + y for y in ys]
    return path + [z * ny for z in reversed(range(nz))]


def form_project_kernel(dims, blocks_ref, *refs):
    shards, row, pool, rank, pairs, block, first_row, last = dims
    g_refs, own_refs, other_refs = (refs[i * shards : (i + 1) * shards] for i in range(3))
    p_hbm, acc_hbm, out_hbm, pbuf, s_ref, held, words, meta, p_sems, acc_sems = refs[3 * shards :]
    blocks = pairs // block
    rows = block * rank
    stride = shards * pool + 8
    room = g_refs[0].shape[1]

    def p_copy(i, h):
        start = pl.multiple_of(first_row + (h * pairs + i * block) * rank, rank)
        return pltpu.make_async_copy(
            p_hbm.at[pl.ds(start, rows)], pbuf.at[i, h], p_sems.at[i, h]
        )

    def acc_rows(k):
        return pl.ds(pl.multiple_of(blocks_ref[row + k] * pool, pool), pool)

    def acc_load(k):
        return pltpu.make_async_copy(
            acc_hbm.at[acc_rows(k)], held.at[pl.ds(k * pool, pool)], acc_sems.at[0, k]
        )

    def acc_store(k):
        return pltpu.make_async_copy(
            held.at[pl.ds(k * pool, pool)], out_hbm.at[acc_rows(k)], acc_sems.at[1, k]
        )

    for i in range(blocks):
        for h in range(2):
            p_copy(i, h).start()
    for k in range(shards):
        acc_load(k).start()
        words[k] = own_refs[k][: 2 * 8, room:].astype(F32).astype(jnp.int32)
    to_scalars = [
        pltpu.make_async_copy(words.at[k, pl.ds(0, 8)], meta.at[k], acc_sems.at[2, k])
        for k in range(shards)
    ]
    for copy in to_scalars:
        copy.start()
    tiles = room // LANES
    low = lax.broadcasted_iota(jnp.int32, (pairs, LANES), 1) < rank
    lane = lax.broadcasted_iota(jnp.int32, (rank, 2 * LANES), 1)
    first_core = jnp.full((rank // 2, 2 * LANES), blocks_ref[blocks_ref.shape[0] - 1]) == 0

    for k in range(shards):
        to_scalars[k].wait()

        def two_examples(p, carry, k=k):
            e = 2 * p
            tile = jnp.minimum(meta[k, 1, e], tiles - 2)
            base = pl.multiple_of(tile * LANES, LANES)
            g = g_refs[k][:, pl.ds(base, 2 * LANES)]
            own = own_refs[k][:, pl.ds(base, 2 * LANES)]
            other = other_refs[k][:, pl.ds(base, 2 * LANES)]
            a = jnp.concatenate(
                [jnp.where(first_core, own, other), jnp.where(first_core, other, own)], axis=0
            )
            masked = []
            for j in range(2):
                begin = meta[k, 1, e + j] * LANES + meta[k, 2, e + j] - base
                end = begin + meta[k, 0, e + j]
                part = jnp.where((lane >= begin) & (lane < end), a, jnp.zeros_like(a))
                masked += [part, part]
            formed = lax.dot_general(
                g,
                jnp.concatenate(masked, axis=0),
                (((1,), (1,)), ((), ())),
                preferred_element_type=F32,
            )
            for j in range(2):
                own = formed[:, j * LANES : (j + 1) * LANES]
                s_ref[pl.ds(k * pool + e + j, pairs, stride=stride), :] = jnp.where(
                    low, own[:pairs], own[pairs:]
                )
            return carry

        lax.fori_loop(0, pool // 2, two_examples, 0, unroll=8 if last else 4)
    for k in range(shards):
        acc_load(k).wait()

    def project(i, carry):
        p_copy(i, 0).wait()
        p_copy(i, 1).wait()
        left = jnp.concatenate(
            [
                s_ref[
                    pl.ds(pl.multiple_of((i * block + o) * stride, 8), shards * pool), :
                ].astype(BF16)
                for o in range(block)
            ],
            axis=1,
        )
        right = jnp.concatenate(
            [
                pbuf[i, h, pl.ds(o * rank, rank), :]
                for o in range(block)
                for h in range(2)
            ],
            axis=0,
        )
        held[...] += jnp.dot(left, right, preferred_element_type=F32)
        return carry

    lax.fori_loop(0, blocks, project, 0, unroll=blocks if last else 1)
    for k in range(shards):
        acc_store(k).start()
    for k in range(shards):
        acc_store(k).wait()


def form_project(acc, blocks, row, gs, acts, projection, half, pool, last):
    shards = len(gs)
    outs = gs[0].shape[0]
    rank = 2 * acts[0][0].shape[0]
    feats = projection.shape[1]
    pairs = outs // 2
    block = min(32, pairs)
    dims = (shards, row, pool, rank, pairs, block, half * outs * rank, last)
    whole = lambda x: pl.BlockSpec(x.shape, lambda i, m: (0, 0))
    flat = list(gs) + [a[0] for a in acts] + [a[1] for a in acts]
    spec = pltpu.PrefetchScalarGridSpec(
        num_scalar_prefetch=1,
        grid=(1,),
        in_specs=[whole(x) for x in flat]
        + [pl.BlockSpec(memory_space=pl.ANY)] * 2,
        out_specs=pl.BlockSpec(memory_space=pl.ANY),
        scratch_shapes=[
            pltpu.VMEM((pairs // block, 2, block * rank, feats), BF16),
            pltpu.VMEM(((pairs + 1) * (shards * pool + 8), LANES), F32),
            pltpu.VMEM((shards * pool, feats), F32),
            pltpu.VMEM((shards, 16, LANES), jnp.int32),
            pltpu.SMEM((shards, 8, LANES), jnp.int32),
            pltpu.SemaphoreType.DMA((pairs // block, 2)),
            pltpu.SemaphoreType.DMA((3, shards)),
        ],
    )
    return pl.pallas_call(
        functools.partial(form_project_kernel, dims),
        out_shape=jax.ShapeDtypeStruct(acc.shape, F32),
        grid_spec=spec,
        input_output_aliases={len(flat) + 2: 0},
        compiler_params=pltpu.CompilerParams(vmem_limit_bytes=VMEM_LIMIT),
        cost_estimate=pl.CostEstimate(
            flops=2 * shards * pool * outs * rank * feats,
            bytes_accessed=outs * rank * feats * 2,
            transcendentals=0,
        ),
        name="form_project",
    )(blocks, *flat, projection, acc)


def exchange_sum(x, axis, n):
    me = lax.axis_index(axis)
    bit = 1
    slots = x[:, None]
    while bit < n:
        swap = [(i, i ^ bit) for i in range(n)]
        mine = (me // bit) % 2
        grouped = slots.reshape((slots.shape[0] // 2, 2) + x.shape[1:])
        keep = lax.dynamic_index_in_dim(grouped, mine, 1, keepdims=False)
        send = lax.dynamic_index_in_dim(grouped, 1 - mine, 1, keepdims=False)
        if bit > 1:
            send = send.astype(BF16)
        slots = keep + lax.ppermute(send, axis, swap).astype(F32)
        bit *= 2
    return slots.reshape(x.shape[1:])


def exchange_total(x, axis, n, bit=1):
    while bit < n:
        x = x + lax.ppermute(x, axis, [(i, i ^ bit) for i in range(n)])
        bit *= 2
    return x


def per_device(dp, fsdp, tokens, grad_rows, down, counts, projection, targets):
    pool, length, width = tokens.shape
    outs = grad_rows.shape[2]
    rank = down.shape[0]
    feats = projection.shape[1]
    half = outs // 2
    room = -(-3 * pool * length // (4 * LANES)) * LANES
    before = jnp.arange(pool)[None, :] < jnp.arange(pool)[:, None]
    starts = jnp.sum(jnp.where(before, counts[None, :], 0), axis=1)
    t = jnp.arange(length, dtype=jnp.int32)[None, :]
    place = jnp.where(t < counts[:, None], starts[:, None] + t, -1).reshape(pool * length)
    select = (place[:, None] == jnp.arange(room, dtype=jnp.int32)[None, :]).astype(BF16)
    packed = lax.dot_general(
        grad_rows.reshape(pool * length, outs),
        select,
        (((0,), (0,)), ((), ())),
        preferred_element_type=F32,
    ).astype(BF16)

    me = lax.axis_index("dp")
    order = ring_order(dp)
    ahead = [(order[i], order[(i + 1) % dp]) for i in range(dp)]
    back = [(b, a) for a, b in ahead]
    swap = [(i, i ^ 1) for i in range(fsdp)]
    core = lax.axis_index("fsdp") % 2

    acts_part = lax.dot_general(
        down,
        tokens.reshape(pool * length, width),
        (((1,), (1,)), ((), ())),
        preferred_element_type=F32,
    ).reshape(2, rank // 2, pool * length)
    keep = lax.dynamic_index_in_dim(acts_part, core, 0, keepdims=False)
    send = lax.dynamic_index_in_dim(acts_part, 1 - core, 0, keepdims=False)
    acts_half = exchange_total(keep + lax.ppermute(send, "fsdp", swap), "fsdp", fsdp, 2)
    real = (place >= 0).astype(F32)[None, :]
    acts_half = (acts_half * real).astype(BF16)

    def both_halves(mine):
        other = lax.ppermute(mine, "fsdp", swap)
        return jnp.where(
            core == 0,
            jnp.concatenate([mine, other], axis=0),
            jnp.concatenate([other, mine], axis=0),
        )

    words = jnp.stack([counts, starts // LANES, starts % LANES]).astype(BF16)
    words = jnp.pad(words, ((0, rank // 2 - 3), (0, -pool % LANES)))
    own_half = jnp.dot(acts_half, select, preferred_element_type=F32).astype(BF16)
    own_half = jnp.concatenate([own_half, words], axis=1)
    my_position = jnp.asarray(np.argsort(order), jnp.int32)[me]
    blocks = jnp.asarray(order, jnp.int32)[(my_position - jnp.arange(dp + 1)) % dp]
    blocks = jnp.concatenate([blocks, core[None].astype(jnp.int32)])

    halves = {0: own_half, dp: own_half}
    acts = {}
    low, high = {0: packed[:half]}, {dp: packed[half:]}
    acc = jnp.zeros((dp * pool, feats), F32)
    overflow = None

    blocks, acc = lax.optimization_barrier((blocks, acc))

    def add(acc, blocks, first, gs, which):
        return form_project(
            acc, blocks, first, [gs[first], gs[first + 1]], [acts[first], acts[first + 1]],
            projection, which, pool, first in (1, dp - 2),
        )

    for s in range(dp):
        keys = [k for k in dict.fromkeys((s, dp - s)) if k in halves and k not in acts]
        if s == dp // 2 + 1:
            used = jnp.stack([halves[i][0, room : room + pool] for i in range(dp)])
            overflow = jnp.max(jnp.sum(used.astype(jnp.int32), axis=1)) > room
            low[s], high[dp - s], acc, overflow = lax.optimization_barrier(
                (low[s], high[dp - s], acc, overflow)
            )
        elif s > 0:
            low[s], high[dp - s], acc, blocks, *fresh = lax.optimization_barrier(
                (low[s], high[dp - s], acc, blocks, *[halves[k] for k in keys])
            )
            halves.update(zip(keys, fresh))
        if s + 1 < dp:
            low[s + 1] = lax.ppermute(low[s], "dp", ahead)
            high[dp - s - 1] = lax.ppermute(high[dp - s], "dp", back)
        if 2 * (s + 1) <= dp:
            halves[s + 1] = lax.ppermute(halves[s], "dp", ahead)
        if 2 * (s + 1) < dp:
            halves[dp - s - 1] = lax.ppermute(halves[dp - s], "dp", back)
        for k in keys:
            acts[k] = acts[0] if k == dp else (halves[k], lax.ppermute(halves[k], "fsdp", swap))
        if s % 2 == 1:
            acc = add(acc, blocks, s - 1, low, 0)
        if s > 0 and s % 2 == 0:
            acc = add(acc, blocks, dp - s + 1, high, 1)
        if s == dp - 1:
            acc = add(acc, blocks, 1, high, 1)

    def padded(acc):
        mine = both_halves(acts_half).reshape(rank, pool, length)
        grads = jnp.einsum("elo,rel->eor", grad_rows, mine, preferred_element_type=F32)
        grads = grads.astype(BF16).reshape(pool, outs * rank)

        def step(s, state):
            acc, grads = state
            part = jnp.dot(grads, projection, preferred_element_type=F32)
            block = lax.dynamic_index_in_dim(blocks, s, 0, keepdims=False)
            acc = lax.dynamic_update_slice(acc, part, (block * pool, 0))
            return acc, lax.ppermute(grads, "dp", ahead)

        return lax.fori_loop(0, dp, step, (acc, grads))[0]

    acc = lax.cond(overflow, padded, lambda acc: acc, acc)
    pooled = exchange_sum(acc.reshape(fsdp, dp * pool // fsdp, feats), "fsdp", fsdp)
    target_f = targets.astype(F32)
    queries = targets.shape[0]
    share = queries // dp
    rows = pooled.shape[0]
    raw = lax.dot_general(
        target_f,
        pooled,
        (((1,), (1,)), ((), ())),
        precision=lax.Precision.HIGHEST,
        preferred_element_type=F32,
    ).reshape(dp, share, rows)
    pool_sq = jnp.sum(pooled * pooled, axis=1)
    target_sq = jnp.sum(target_f * target_f, axis=1).reshape(dp, 1, share)
    sent = jnp.concatenate(
        [
            raw,
            jnp.broadcast_to(pool_sq[None, None, :], (dp, 1, rows)),
            jnp.pad(target_sq, ((0, 0), (0, 0), (0, rows - share))),
        ],
        axis=1,
    )
    got = jnp.sum(lax.all_to_all(sent, "dp", 0, 0), axis=0)
    pool_norm = jnp.sqrt(got[share] + 1e-06)
    target_norm = jnp.sqrt(got[share + 1, :share] + 1e-06)
    scale = jnp.sqrt(F32(feats * dp))
    return (got[:share].T / pool_norm[:, None]) / target_norm[None, :] * scale


def solution(mesh):
    dp, fsdp = mesh.shape["dp"], mesh.shape["fsdp"]
    return jax.shard_map(
        functools.partial(per_device, dp, fsdp),
        mesh=mesh,
        in_specs=(
            P("dp", None, "fsdp"),
            P("dp", None, "fsdp"),
            P(None, "fsdp"),
            P("dp"),
            P("fsdp", "dp"),
            P(None, "dp"),
        ),
        out_specs=P("fsdp", "dp"),
        check_vma=False,
    )
```

```python
import functools

import jax
import jax.numpy as jnp
import numpy as np
from jax import lax
from jax.experimental import pallas as pl
from jax.experimental.pallas import tpu as pltpu
from jax.sharding import PartitionSpec as P

F32 = jnp.float32
BF16 = jnp.bfloat16
LANES = 128
VMEM_LIMIT = 31 * 1024 * 1024


def ring_order(n):
    ny = 2
    while ny * ny * 4 <= n:
        ny *= 2
    nz = n // ny
    path = []
    for z in range(nz):
        ys = range(1, ny) if z % 2 == 0 else range(ny - 1, 0, -1)
        path += [z * ny + y for y in ys]
    return path + [z * ny for z in reversed(range(nz))]


def form_project_kernel(dims, blocks_ref, *refs):
    shards, row, pool, rank, pairs, block, first_row, last = dims
    g_refs, own_refs, other_refs = (refs[i * shards : (i + 1) * shards] for i in range(3))
    p_hbm, acc_hbm, out_hbm, pbuf, s_ref, held, words, meta, p_sems, acc_sems = refs[3 * shards :]
    blocks = pairs // block
    rows = block * rank
    stride = shards * pool + 8
    room = g_refs[0].shape[1]

    def p_copy(i, h):
        start = pl.multiple_of(first_row + (h * pairs + i * block) * rank, rank)
        return pltpu.make_async_copy(
            p_hbm.at[pl.ds(start, rows)], pbuf.at[i, h], p_sems.at[i, h]
        )

    def acc_rows(k):
        return pl.ds(pl.multiple_of(blocks_ref[row + k] * pool, pool), pool)

    def acc_load(k):
        return pltpu.make_async_copy(
            acc_hbm.at[acc_rows(k)], held.at[pl.ds(k * pool, pool)], acc_sems.at[0, k]
        )

    def acc_store(k):
        return pltpu.make_async_copy(
            held.at[pl.ds(k * pool, pool)], out_hbm.at[acc_rows(k)], acc_sems.at[1, k]
        )

    for i in range(blocks):
        for h in range(2):
            p_copy(i, h).start()
    for k in range(shards):
        acc_load(k).start()
        words[k] = own_refs[k][: 2 * 8, room:].astype(F32).astype(jnp.int32)
    to_scalars = [
        pltpu.make_async_copy(words.at[k, pl.ds(0, 8)], meta.at[k], acc_sems.at[2, k])
        for k in range(shards)
    ]
    for copy in to_scalars:
        copy.start()
    tiles = room // LANES
    low = lax.broadcasted_iota(jnp.int32, (pairs, LANES), 1) < rank
    lane = lax.broadcasted_iota(jnp.int32, (rank, 2 * LANES), 1)
    first_core = jnp.full((rank // 2, 2 * LANES), blocks_ref[blocks_ref.shape[0] - 1]) == 0

    for k in range(shards):
        to_scalars[k].wait()

        def two_examples(p, carry, k=k):
            e = 2 * p
            tile = jnp.minimum(meta[k, 1, e], tiles - 2)
            base = pl.multiple_of(tile * LANES, LANES)
            g = g_refs[k][:, pl.ds(base, 2 * LANES)]
            own = own_refs[k][:, pl.ds(base, 2 * LANES)]
            other = other_refs[k][:, pl.ds(base, 2 * LANES)]
            a = jnp.concatenate(
                [jnp.where(first_core, own, other), jnp.where(first_core, other, own)], axis=0
            )
            masked = []
            for j in range(2):
                begin = meta[k, 1, e + j] * LANES + meta[k, 2, e + j] - base
                end = begin + meta[k, 0, e + j]
                part = jnp.where((lane >= begin) & (lane < end), a, jnp.zeros_like(a))
                masked += [part, part]
            formed = lax.dot_general(
                g,
                jnp.concatenate(masked, axis=0),
                (((1,), (1,)), ((), ())),
                preferred_element_type=F32,
            )
            for j in range(2):
                own = formed[:, j * LANES : (j + 1) * LANES]
                s_ref[pl.ds(k * pool + e + j, pairs, stride=stride), :] = jnp.where(
                    low, own[:pairs], own[pairs:]
                )
            return carry

        lax.fori_loop(0, pool // 2, two_examples, 0, unroll=8 if last else 4)
    for k in range(shards):
        acc_load(k).wait()

    def project(i, carry):
        p_copy(i, 0).wait()
        p_copy(i, 1).wait()
        left = jnp.concatenate(
            [
                s_ref[
                    pl.ds(pl.multiple_of((i * block + o) * stride, 8), shards * pool), :
                ].astype(BF16)
                for o in range(block)
            ],
            axis=1,
        )
        right = jnp.concatenate(
            [
                pbuf[i, h, pl.ds(o * rank, rank), :]
                for o in range(block)
                for h in range(2)
            ],
            axis=0,
        )
        held[...] += jnp.dot(left, right, preferred_element_type=F32)
        return carry

    lax.fori_loop(0, blocks, project, 0, unroll=blocks if last else 1)
    for k in range(shards):
        acc_store(k).start()
    for k in range(shards):
        acc_store(k).wait()


def form_project(acc, blocks, row, gs, acts, projection, half, pool, last):
    shards = len(gs)
    outs = gs[0].shape[0]
    rank = 2 * acts[0][0].shape[0]
    feats = projection.shape[1]
    pairs = outs // 2
    block = min(32, pairs)
    dims = (shards, row, pool, rank, pairs, block, half * outs * rank, last)
    whole = lambda x: pl.BlockSpec(x.shape, lambda i, m: (0, 0))
    flat = list(gs) + [a[0] for a in acts] + [a[1] for a in acts]
    spec = pltpu.PrefetchScalarGridSpec(
        num_scalar_prefetch=1,
        grid=(1,),
        in_specs=[whole(x) for x in flat]
        + [pl.BlockSpec(memory_space=pl.ANY)] * 2,
        out_specs=pl.BlockSpec(memory_space=pl.ANY),
        scratch_shapes=[
            pltpu.VMEM((pairs // block, 2, block * rank, feats), BF16),
            pltpu.VMEM(((pairs + 1) * (shards * pool + 8), LANES), F32),
            pltpu.VMEM((shards * pool, feats), F32),
            pltpu.VMEM((shards, 16, LANES), jnp.int32),
            pltpu.SMEM((shards, 8, LANES), jnp.int32),
            pltpu.SemaphoreType.DMA((pairs // block, 2)),
            pltpu.SemaphoreType.DMA((3, shards)),
        ],
    )
    return pl.pallas_call(
        functools.partial(form_project_kernel, dims),
        out_shape=jax.ShapeDtypeStruct(acc.shape, F32),
        grid_spec=spec,
        input_output_aliases={len(flat) + 2: 0},
        compiler_params=pltpu.CompilerParams(vmem_limit_bytes=VMEM_LIMIT),
        cost_estimate=pl.CostEstimate(
            flops=2 * shards * pool * outs * rank * feats,
            bytes_accessed=outs * rank * feats * 2,
            transcendentals=0,
        ),
        name="form_project",
    )(blocks, *flat, projection, acc)


def exchange_sum(x, axis, n):
    me = lax.axis_index(axis)
    bit = 1
    slots = x[:, None]
    while bit < n:
        swap = [(i, i ^ bit) for i in range(n)]
        mine = (me // bit) % 2
        grouped = slots.reshape((slots.shape[0] // 2, 2) + x.shape[1:])
        keep = lax.dynamic_index_in_dim(grouped, mine, 1, keepdims=False)
        send = lax.dynamic_index_in_dim(grouped, 1 - mine, 1, keepdims=False)
        if bit > 1:
            send = send.astype(BF16)
        slots = keep + lax.ppermute(send, axis, swap).astype(F32)
        bit *= 2
    return slots.reshape(x.shape[1:])


def exchange_total(x, axis, n, bit=1):
    while bit < n:
        x = x + lax.ppermute(x, axis, [(i, i ^ bit) for i in range(n)])
        bit *= 2
    return x


def per_device(dp, fsdp, tokens, grad_rows, down, counts, projection, targets):
    pool, length, width = tokens.shape
    outs = grad_rows.shape[2]
    rank = down.shape[0]
    feats = projection.shape[1]
    half = outs // 2
    room = -(-3 * pool * length // (4 * LANES)) * LANES
    before = jnp.arange(pool)[None, :] < jnp.arange(pool)[:, None]
    starts = jnp.sum(jnp.where(before, counts[None, :], 0), axis=1)
    t = jnp.arange(length, dtype=jnp.int32)[None, :]
    place = jnp.where(t < counts[:, None], starts[:, None] + t, -1).reshape(pool * length)
    select = (place[:, None] == jnp.arange(room, dtype=jnp.int32)[None, :]).astype(BF16)
    packed = lax.dot_general(
        grad_rows.reshape(pool * length, outs),
        select,
        (((0,), (0,)), ((), ())),
        preferred_element_type=F32,
    ).astype(BF16)

    me = lax.axis_index("dp")
    order = ring_order(dp)
    ahead = [(order[i], order[(i + 1) % dp]) for i in range(dp)]
    back = [(b, a) for a, b in ahead]
    swap = [(i, i ^ 1) for i in range(fsdp)]
    core = lax.axis_index("fsdp") % 2

    acts_part = lax.dot_general(
        down,
        tokens.reshape(pool * length, width),
        (((1,), (1,)), ((), ())),
        preferred_element_type=F32,
    ).reshape(2, rank // 2, pool * length)
    keep = lax.dynamic_index_in_dim(acts_part, core, 0, keepdims=False)
    send = lax.dynamic_index_in_dim(acts_part, 1 - core, 0, keepdims=False)
    acts_half = exchange_total(keep + lax.ppermute(send, "fsdp", swap), "fsdp", fsdp, 2)
    real = (place >= 0).astype(F32)[None, :]
    acts_half = (acts_half * real).astype(BF16)

    def both_halves(mine):
        other = lax.ppermute(mine, "fsdp", swap)
        return jnp.where(
            core == 0,
            jnp.concatenate([mine, other], axis=0),
            jnp.concatenate([other, mine], axis=0),
        )

    words = jnp.stack([counts, starts // LANES, starts % LANES]).astype(BF16)
    words = jnp.pad(words, ((0, rank // 2 - 3), (0, -pool % LANES)))
    own_half = jnp.dot(acts_half, select, preferred_element_type=F32).astype(BF16)
    own_half = jnp.concatenate([own_half, words], axis=1)
    my_position = jnp.asarray(np.argsort(order), jnp.int32)[me]
    blocks = jnp.asarray(order, jnp.int32)[(my_position - jnp.arange(dp + 1)) % dp]
    blocks = jnp.concatenate([blocks, core[None].astype(jnp.int32)])

    halves = {0: own_half, dp: own_half}
    acts = {}
    low, high = {0: packed[:half]}, {dp: packed[half:]}
    acc = jnp.zeros((dp * pool, feats), F32)
    overflow = None

    blocks, acc = lax.optimization_barrier((blocks, acc))

    def add(acc, blocks, first, gs, which):
        return form_project(
            acc, blocks, first, [gs[first], gs[first + 1]], [acts[first], acts[first + 1]],
            projection, which, pool, first in (1, dp - 2),
        )

    for s in range(dp):
        keys = [k for k in dict.fromkeys((s, dp - s)) if k in halves and k not in acts]
        if s == dp // 2 + 1:
            used = jnp.stack([halves[i][0, room : room + pool] for i in range(dp)])
            overflow = jnp.max(jnp.sum(used.astype(jnp.int32), axis=1)) > room
            low[s], high[dp - s], acc, overflow = lax.optimization_barrier(
                (low[s], high[dp - s], acc, overflow)
            )
        elif s > 0:
            low[s], high[dp - s], acc, blocks, *fresh = lax.optimization_barrier(
                (low[s], high[dp - s], acc, blocks, *[halves[k] for k in keys])
            )
            halves.update(zip(keys, fresh))
        if s + 1 < dp:
            low[s + 1] = lax.ppermute(low[s], "dp", ahead)
            high[dp - s - 1] = lax.ppermute(high[dp - s], "dp", back)
        if 2 * (s + 1) <= dp:
            halves[s + 1] = lax.ppermute(halves[s], "dp", ahead)
        if 2 * (s + 1) < dp:
            halves[dp - s - 1] = lax.ppermute(halves[dp - s], "dp", back)
        for k in keys:
            acts[k] = acts[0] if k == dp else (halves[k], lax.ppermute(halves[k], "fsdp", swap))
        if s % 2 == 1:
            acc = add(acc, blocks, s - 1, low, 0)
        if s > 0 and s % 2 == 0:
            acc = add(acc, blocks, dp - s + 1, high, 1)
        if s == dp - 1:
            acc = add(acc, blocks, 1, high, 1)

    def padded(acc):
        mine = both_halves(acts_half).reshape(rank, pool, length)
        grads = jnp.einsum("elo,rel->eor", grad_rows, mine, preferred_element_type=F32)
        grads = grads.astype(BF16).reshape(pool, outs * rank)

        def step(s, state):
            acc, grads = state
            part = jnp.dot(grads, projection, preferred_element_type=F32)
            block = lax.dynamic_index_in_dim(blocks, s, 0, keepdims=False)
            acc = lax.dynamic_update_slice(acc, part, (block * pool, 0))
            return acc, lax.ppermute(grads, "dp", ahead)

        return lax.fori_loop(0, dp, step, (acc, grads))[0]

    acc = lax.cond(overflow, padded, lambda acc: acc, acc)
    pooled = exchange_sum(acc.reshape(fsdp, dp * pool // fsdp, feats), "fsdp", fsdp)
    target_f = targets.astype(F32)
    queries = targets.shape[0]
    share = queries // dp
    rows = pooled.shape[0]
    raw = lax.dot_general(
        target_f,
        pooled,
        (((1,), (1,)), ((), ())),
        precision=lax.Precision.HIGHEST,
        preferred_element_type=F32,
    ).reshape(dp, share, rows)
    pool_sq = jnp.sum(pooled * pooled, axis=1)
    target_sq = jnp.sum(target_f * target_f, axis=1).reshape(dp, 1, share)
    sent = jnp.concatenate(
        [
            raw,
            jnp.broadcast_to(pool_sq[None, None, :], (dp, 1, rows)),
            jnp.pad(target_sq, ((0, 0), (0, 0), (0, rows - share))),
        ],
        axis=1,
    )
    got = jnp.sum(lax.all_to_all(sent, "dp", 0, 0), axis=0)
    pool_norm = jnp.sqrt(got[share] + 1e-06)
    target_norm = jnp.sqrt(got[share + 1, :share] + 1e-06)
    scale = jnp.sqrt(F32(feats * dp))
    return (got[:share].T / pool_norm[:, None]) / target_norm[None, :] * scale


def solution(mesh):
    dp, fsdp = mesh.shape["dp"], mesh.shape["fsdp"]
    return jax.shard_map(
        functools.partial(per_device, dp, fsdp),
        mesh=mesh,
        in_specs=(
            P("dp", None, "fsdp"),
            P("dp", None, "fsdp"),
            P(None, "fsdp"),
            P("dp"),
            P("fsdp", "dp"),
            P(None, "dp"),
        ),
        out_specs=P("fsdp", "dp"),
        check_vma=False,
    )
```
